32 devices in a mesh: freq: 4 (over y, core), src: 8 (over z, x).
Axes of the slice: x: 2, y: 2, z: 4, core: 2. Of those that a mesh axis runs over, the one named last changes fastest.
Arguments:
- spectra: bfloat16 [8, 2, 306, 512], P('freq', None, None, 'src'), may hold values from -200 to 200
- keep: int32 [512], P('src'), may hold values from 0 to 1, as said below
- lead_field: float32 [3, 306, 2048], P(None, None, 'src'), may hold values from -0.625 to 0.625
- parcel: int32 [2048], P('src'), may hold values from 0 to 67, never falling along the last dimension, each value on 1 to 61 neighbouring positions
Outputs:
- source_power: float32 [8, 2048], P('freq', 'src')
- parcel_power: float32 [8, 68], P('freq')
The draws below stay inside these ranges and needn't reach their ends.
Inputs may be any that keep to these rules, and one draw needn't show every extreme that they name: `keep`: at least 8 epochs are kept.
All inputs are finite; a program needn't handle non-finite values.
Results may differ from the reference program's by a relative error of at most 0.0003.
Values sent between devices are 32-bit elements; how exact they have to be, the bound alone decides.
A program may use at most 64 MiB of HBM per device.

```python
import math
import jax
import jax.numpy as jnp
import numpy as np
from jax import lax

CH = 306
PARCELS = 68
FREQS = 8
EPOCHS = 512
SOURCES = 2048


def draw_spectra(key, part):
    base_key = jax.random.fold_in(key, 11)
    first_key, chan_key, amp_key = jax.random.split(base_key, 3)
    shape = (FREQS, 2, CH, EPOCHS)
    base = jnp.clip(jax.random.normal(first_key, shape, jnp.float32), -5.0, 5.0)
    mixed = base + 0.6 * jnp.roll(base, 1, axis=2) - 0.4 * jnp.roll(base, 7, axis=2)
    channel_scale = jnp.exp(jax.random.uniform(chan_key, (1, 1, CH, 1), jnp.float32, math.log(0.3), math.log(3.0)))
    ramp = jnp.exp(jnp.linspace(0.0, math.log(3.0), FREQS).astype(jnp.float32))
    amplitude = ramp * jnp.exp(jax.random.uniform(amp_key, (FREQS,), jnp.float32, -0.35, 0.35))
    return (mixed * channel_scale * amplitude[:, None, None, None]).astype(jnp.bfloat16)


def draw_keep(key, part):
    position = jnp.arange(EPOCHS, dtype=jnp.int32)
    ticket = jax.random.randint(jax.random.fold_in(key, 23), (EPOCHS,), 0, 1000, dtype=jnp.int32)
    threshold = 300 + 600 * position // EPOCHS
    chosen = (ticket < threshold).astype(jnp.int32)
    return jnp.where(position % 64 == 63, 1, chosen).astype(jnp.int32)


def steps_of(rng, dims, pieces, least, top_value):
    def one(dim, blocks):
        draws = jax.random.uniform(jax.random.fold_in(jax.random.fold_in(rng, 6), dim), (blocks,), jnp.float32, least / len(pieces), top_value / len(pieces))
        return jnp.repeat(jnp.exp(draws), dims[dim] // blocks).reshape((-1,) + (1,) * (len(dims) - dim - 1))

    level = one(*pieces[0])
    for cut in pieces[1:]:
        level = level * one(*cut)
    return level


def split_up(count, total, reach, lean):
    portions = [(1 << 20) // math.isqrt(standing ** lean) + 1 for standing in range(2, count + 1)]
    surplus, holding = total - reach - (count - 1), [1] * (count - 1)
    while surplus > 0:
        candidates = [i for i in range(count - 1) if holding[i] < reach]
        pool, budget = sum([portions[i] for i in candidates]), surplus
        for i in candidates:
            addition = min(reach - holding[i], max(1, budget * portions[i] // pool), surplus)
            holding[i] = holding[i] + addition
            surplus = surplus - addition
    return np.array([reach] + holding)


def ragged(key, count, total, bound, slope):
    if count == 2:
        one = jax.random.randint(key, (), max(1, total - bound), min(bound, total - 1) + 1)
        return jnp.stack([one, total - one])
    sizes = jnp.asarray(split_up(count, total, bound, slope), jnp.int32)
    twos = (count - 1) // 2
    giver, sink = sizes[1:1 + 2 * twos:2], sizes[2:2 + 2 * twos:2]
    room = jnp.minimum(giver - 1, bound - sink)
    passed = jax.random.randint(jax.random.fold_in(key, 1), (twos,), 0, 1 << 20) % (room + 1)
    sizes = sizes.at[1:1 + 2 * twos:2].set(giver - passed).at[2:2 + 2 * twos:2].set(sink + passed)
    return sizes[jax.random.permutation(jax.random.fold_in(key, 2), count)]


def centred(own_key, shape, scale, limit, cuts=(), kind=jnp.bfloat16):
    level = steps_of(own_key, shape, cuts, -0.22, 0.18) if cuts else 1.0
    values = jax.random.normal(own_key, shape, jnp.float32) * scale * level
    return jnp.minimum(jnp.maximum(values, -limit), limit).astype(kind)


def setup_inputs(seed: int = 0) -> dict:
    splits = jax.random.split(jax.random.key(seed), 5)
    return {
        "spectra": draw_spectra(jax.random.fold_in(splits[4], 71), 0),
        "keep": draw_keep(jax.random.fold_in(splits[4], 71), 0),
        "lead_field": centred(splits[2], (3, CH, SOURCES), (CH // 3) ** -0.5, 0.625, ((2, 8),), jnp.float32),
        "parcel": jnp.searchsorted(jnp.cumsum(ragged(splits[3], PARCELS, SOURCES, 2 * SOURCES // PARCELS + 1, 1)), jnp.arange(SOURCES), side="right").astype(jnp.int32),
    }


ridge = 0.05

def inverse_trace(gram):
    gram_xx = gram[..., 0, 0, :]
    gram_xy = gram[..., 0, 1, :]
    gram_xz = gram[..., 0, 2, :]
    gram_yy = gram[..., 1, 1, :]
    gram_yz = gram[..., 1, 2, :]
    gram_zz = gram[..., 2, 2, :]
    minor_xx = gram_yy * gram_zz - gram_yz * gram_yz
    minor_yy = gram_xx * gram_zz - gram_xz * gram_xz
    minor_zz = gram_xx * gram_yy - gram_xy * gram_xy
    determinant = gram_xx * minor_xx - gram_xy * (gram_xy * gram_zz - gram_yz * gram_xz) + gram_xz * (gram_xy * gram_yz - gram_yy * gram_xz)
    return (minor_xx + minor_yy + minor_zz) / determinant

def regularize(summed, kept_total):
    channels = summed.shape[-1]
    spectral = summed / kept_total
    trace_sum = jnp.trace(spectral, axis1=-2, axis2=-1)
    identity = jnp.eye(channels, dtype=summed.dtype)
    return spectral + (ridge * trace_sum / channels)[..., None, None] * identity

def reference(spectra, keep, lead_field, parcel):
    kept_total = jnp.sum(keep).astype(jnp.float32)
    masked = spectra * keep.astype(spectra.dtype)
    columns = jnp.transpose(lead_field, (1, 0, 2)).reshape(CH, 3 * SOURCES)

    def per_bin(block):
        widened = block.astype(jnp.float32)
        summed = jnp.einsum('pce,pde->cd', widened, widened, precision=lax.Precision.HIGHEST)
        factor = jnp.linalg.cholesky(regularize(summed, kept_total))
        whitened = jax.scipy.linalg.solve_triangular(factor, columns, lower=True).reshape(CH, 3, SOURCES)
        gram = jnp.einsum('cos,cqs->oqs', whitened, whitened, precision=lax.Precision.HIGHEST)
        return inverse_trace(gram)
    source_power = lax.map(per_bin, masked)
    bin_mean = jnp.mean(source_power, axis=0)
    relative = source_power / bin_mean
    onehot = (parcel[:, None] == jnp.arange(PARCELS, dtype=jnp.int32)[None, :]).astype(jnp.float32)
    sums = jnp.dot(relative, onehot, precision=lax.Precision.HIGHEST)
    members = jnp.sum(onehot, axis=0)
    return (source_power, sums / members)
```

```python
import functools
import jax
import jax.numpy as jnp
from jax import lax
from jax.experimental import pallas as pl
from jax.experimental.pallas import tpu as pltpu
from jax.sharding import PartitionSpec as P

PARCELS = 68
ridge = 0.05
MESH = pl.DeviceIdType.MESH
HI = lax.Precision.HIGHEST
LANES = 128


def block_plan(rows):
    sizes = [min(LANES, rows - at) for at in range(0, rows, LANES)]
    offsets, total = {}, 0
    for i, size in enumerate(sizes):
        for j in range(i + 1):
            offsets[i, j] = total
            total += size // 8
    return sizes, offsets, total


def cov_kernel(n, chunk, x_ref, out_ref, packed, landing, gathered, send, recv, send2, recv2):
    bins, rows, _ = x_ref.shape
    sizes, offsets, total = block_plan(rows)
    me = lax.axis_index("src")
    barrier = pltpu.get_barrier_semaphore()
    for d in range(1, n):
        pl.semaphore_signal(barrier, inc=1, device_id={"src": lax.rem(me + d, n)}, device_id_type=MESH)
    for f in range(bins):
        for i, size in enumerate(sizes):
            left = x_ref[f, i * LANES : i * LANES + size, :]
            for j in range(i + 1):
                width = sizes[j]
                right = x_ref[f, j * LANES : j * LANES + width, :]
                block = lax.dot_general(left, right, (((1,), (1,)), ((), ())), preferred_element_type=jnp.float32)
                if width < LANES:
                    block = jnp.concatenate([block, jnp.zeros((size, LANES - width), jnp.float32)], axis=1)
                at = f * total + offsets[i, j]
                packed[at : at + size // 8] = block.reshape(size // 8, 8, LANES)
    spare = n * chunk - bins * total
    if spare:
        packed[bins * total :] = jnp.zeros((spare, 8, LANES), jnp.float32)
    pl.semaphore_wait(barrier, n - 1)
    copies = []
    for d in range(1, n):
        to = lax.rem(me + d, n)
        copy = pltpu.make_async_remote_copy(
            src_ref=packed.at[pl.ds(to * chunk, chunk)],
            dst_ref=landing.at[d],
            send_sem=send.at[d],
            recv_sem=recv.at[d],
            device_id={"src": to},
            device_id_type=MESH,
        )
        copy.start()
        copies.append(copy)
    acc = packed[pl.ds(me * chunk, chunk)]
    for d in range(1, n):
        copies[d - 1].wait_recv()
        acc = acc + landing[d]
    gathered[pl.ds(me * chunk, chunk)] = acc
    again = []
    for d in range(1, n):
        to = lax.rem(me + d, n)
        copy = pltpu.make_async_remote_copy(
            src_ref=gathered.at[pl.ds(me * chunk, chunk)],
            dst_ref=gathered.at[pl.ds(me * chunk, chunk)],
            send_sem=send2.at[d],
            recv_sem=recv2.at[d],
            device_id={"src": to},
            device_id_type=MESH,
        )
        copy.start()
        again.append(copy)
    for d in range(1, n):
        again[d - 1].wait_recv()
    for d in range(1, n):
        copies[d - 1].wait_send()
        again[d - 1].wait_send()
    out_ref[...] = gathered[...]


def summed_cov(x, n):
    bins, rows, _ = x.shape
    total = block_plan(rows)[2] * bins
    chunk = -(-total // n)
    full = (n * chunk, 8, LANES)
    return pl.pallas_call(
        functools.partial(cov_kernel, n, chunk),
        out_shape=jax.ShapeDtypeStruct(full, jnp.float32),
        in_specs=[pl.BlockSpec(memory_space=pltpu.VMEM)],
        out_specs=pl.BlockSpec(memory_space=pltpu.VMEM),
        scratch_shapes=[
            pltpu.VMEM(full, jnp.float32),
            pltpu.VMEM((n, chunk, 8, LANES), jnp.float32),
            pltpu.VMEM(full, jnp.float32),
            pltpu.SemaphoreType.DMA((n,)),
            pltpu.SemaphoreType.DMA((n,)),
            pltpu.SemaphoreType.DMA((n,)),
            pltpu.SemaphoreType.DMA((n,)),
        ],
        compiler_params=pltpu.CompilerParams(collective_id=0, has_side_effects=True),
        name="cov_exchange",
    )(x)


def split3(x):
    high = x.astype(jnp.bfloat16).astype(jnp.float32)
    rest = x - high
    middle = rest.astype(jnp.bfloat16).astype(jnp.float32)
    return high, middle, rest - middle


def panel(p):
    lane = lax.broadcasted_iota(jnp.int32, (8, LANES), 1)
    row = lax.broadcasted_iota(jnp.int32, (8, LANES), 0)
    for k in range(8):
        col = jnp.broadcast_to(p[:, k : k + 1], (8, LANES))
        pivot = jnp.broadcast_to(col[k : k + 1, :], (8, LANES))
        line = jnp.where(lane == k, 1.0, jnp.broadcast_to(p[k : k + 1, :], (8, LANES)))
        scale = lax.rsqrt(pivot)
        scale = scale * (1.5 - 0.5 * pivot * scale * scale)
        line = line * scale
        step = jnp.where(row > k, col * scale, 0.0)
        p = jnp.where(row == k, line, jnp.where((lane == k) & (row > k), 0.0, p) - step * line)
    return jnp.where((lane < 8) & (lane > row), 0.0, p)


def invert_factors(work, bins, size):
    lane = lax.broadcasted_iota(jnp.int32, (8, LANES), 1)
    rest_lane = lax.broadcasted_iota(jnp.int32, (size - 8, LANES), 1)

    def body(t, carry):
        for f in range(bins):
            u = panel(work[f, 0:8, :])
            ahead = jnp.where((lane >= 8) & (lane < size - 8 * t), u, 0.0)
            ah, am, al = split3(ahead)
            uh, um, ul = split3(u)
            left = jnp.concatenate([ah, ah, am, ah, am, al], axis=0).astype(jnp.bfloat16)
            right = jnp.concatenate([uh, um, uh, ul, um, uh], axis=0).astype(jnp.bfloat16)
            update = lax.dot_general(left, right, (((0,), (0,)), ((), ())), preferred_element_type=jnp.float32)
            below = jnp.where(rest_lane < 8, 0.0, work[f, 8:size, :]) - update[8:size, :]
            work[f, 0 : size - 8, :] = pltpu.roll(below, LANES - 8, axis=1)
            work[f, size - 8 : size, :] = pltpu.roll(u, LANES - 8, axis=1)
        return carry

    lax.fori_loop(0, size // 8, body, 0)
    if size < LANES:
        for f in range(bins):
            work[f, 0:size, :] = pltpu.roll(work[f, 0:size, :], size, axis=1)


def dot(a, b):
    return jnp.dot(a, b, precision=HI, preferred_element_type=jnp.float32)


def dot_t(a, b):
    return lax.dot_general(a, b, (((1,), (1,)), ((), ())), precision=HI, preferred_element_type=jnp.float32)


def solve_kernel(bins, packed_ref, lead_ref, out_ref, blocks, work, white, tail):
    channels, sources = lead_ref.shape[1], lead_ref.shape[2]
    rows = blocks_rows(channels)
    sizes, offsets, total = block_plan(rows)
    count = len(sizes)
    for f in range(bins):
        def raw(i, j):
            at = f * total + offsets[i, j]
            return packed_ref[at : at + sizes[i] // 8].reshape(sizes[i], LANES)

        spot = f * total + offsets[count - 1, count - 1]
        edge = channels - (count - 1) * LANES
        kept = packed_ref[spot + edge // 8][edge % 8 : edge % 8 + 1, edge : edge + 1]
        inverse_kept = 1.0 / kept
        eyes, trace = [], jnp.zeros((1, 1), jnp.float32)
        for i, size in enumerate(sizes):
            r = lax.broadcasted_iota(jnp.int32, (size, LANES), 0)
            c = lax.broadcasted_iota(jnp.int32, (size, LANES), 1)
            inside = r + i * LANES < channels
            diagonal = jnp.where((r == c) & inside, raw(i, i), 0.0)
            trace = trace + jnp.sum(jnp.sum(diagonal, axis=0, keepdims=True), axis=1, keepdims=True)
        add = ridge * (trace * inverse_kept) / channels
        for i, size in enumerate(sizes):
            r = lax.broadcasted_iota(jnp.int32, (size, LANES), 0)
            c = lax.broadcasted_iota(jnp.int32, (size, LANES), 1)
            inside = r + i * LANES < channels
            for j in range(i + 1):
                value = raw(i, j) * inverse_kept
                value = jnp.where(inside & (c + j * LANES < channels), value, 0.0)
                if i == j:
                    value = value + jnp.where(r == c, jnp.where(inside, add, 1.0), 0.0)
                blocks[f, i, j, 0:size, :] = value

    tail[...] = jnp.zeros_like(tail)
    for o in range(3):
        tail[0 : channels - (count - 1) * LANES, o * sources : (o + 1) * sources] = lead_ref[o, (count - 1) * LANES : channels, :]

    def lead_block(i):
        if i == count - 1:
            return tail[...]
        return jnp.concatenate([lead_ref[o, i * LANES : (i + 1) * LANES, :] for o in range(3)], axis=1)

    for i, size in enumerate(sizes):
        for f in range(bins):
            work[f, 0:size, :] = blocks[f, i, i, 0:size, :]
        invert_factors(work, bins, size)
        for f in range(bins):
            inverse = work[f, 0:size, 0:size]
            for j in range(i + 1, count):
                blocks[f, j, i, 0 : sizes[j], :] = dot_t(blocks[f, j, i, 0 : sizes[j], :], inverse)
            for j in range(i + 1, count):
                for k in range(i + 1, j + 1):
                    low, high = blocks[f, j, i, 0 : sizes[j], :], blocks[f, k, i, 0 : sizes[k], :]
                    blocks[f, j, k, 0 : sizes[j], 0 : sizes[k]] = blocks[f, j, k, 0 : sizes[j], 0 : sizes[k]] - dot_t(low, high)
            column = lead_block(i)
            for j in range(i):
                column = column - dot(blocks[f, i, j, 0:size, :], white[f, j * LANES : (j + 1) * LANES, :])
            white[f, i * LANES : i * LANES + size, :] = dot(inverse, column)
    for f in range(bins):
        gram = {}
        for a in range(3):
            for b in range(a, 3):
                wa = white[f, :, a * sources : (a + 1) * sources]
                wb = white[f, :, b * sources : (b + 1) * sources]
                gram[a, b] = jnp.sum(wa * wb, axis=0, keepdims=True)
        xx, xy, xz, yy, yz, zz = gram[0, 0], gram[0, 1], gram[0, 2], gram[1, 1], gram[1, 2], gram[2, 2]
        minor_xx = yy * zz - yz * yz
        minor_yy = xx * zz - xz * xz
        minor_zz = xx * yy - xy * xy
        determinant = xx * minor_xx - xy * (xy * zz - yz * xz) + xz * (xy * yz - yy * xz)
        out_ref[f : f + 1, :] = (minor_xx + minor_yy + minor_zz) / determinant


def blocks_rows(channels):
    return -(-(channels + 1) // 16) * 16


def solve(packed, lead_field, bins):
    channels, sources = lead_field.shape[1:]
    rows = blocks_rows(channels)
    sizes, _, _ = block_plan(rows)
    count = len(sizes)
    return pl.pallas_call(
        functools.partial(solve_kernel, bins),
        out_shape=jax.ShapeDtypeStruct((bins, sources), jnp.float32),
        in_specs=[pl.BlockSpec(memory_space=pltpu.VMEM)] * 2,
        out_specs=pl.BlockSpec(memory_space=pltpu.VMEM),
        scratch_shapes=[
            pltpu.VMEM((bins, count, count, LANES, LANES), jnp.float32),
            pltpu.VMEM((bins, LANES, LANES), jnp.float32),
            pltpu.VMEM((bins, rows, 3 * sources), jnp.float32),
            pltpu.VMEM((sizes[-1], 3 * sources), jnp.float32),
        ],
        name="factor_whiten",
    )(packed, lead_field)


def parcel_kernel(nf, ns, power_ref, parcel_ref, out_ref, mine, bin_land, part, part_land, send_f, recv_f, send_s, recv_s):
    bins, sources = power_ref.shape
    mf, ms = lax.axis_index("freq"), lax.axis_index("src")
    barrier = pltpu.get_barrier_semaphore()
    for d in range(1, nf):
        pl.semaphore_signal(barrier, inc=1, device_id={"freq": lax.rem(mf + d, nf)}, device_id_type=MESH)
    for d in range(1, ns):
        pl.semaphore_signal(barrier, inc=1, device_id={"src": lax.rem(ms + d, ns)}, device_id_type=MESH)
    power = power_ref[...]
    here = jnp.sum(power, axis=0, keepdims=True)
    mine[...] = jnp.broadcast_to(here, mine.shape)
    pl.semaphore_wait(barrier, nf + ns - 2)
    copies = []
    for d in range(1, nf):
        copy = pltpu.make_async_remote_copy(
            src_ref=mine,
            dst_ref=bin_land.at[d],
            send_sem=send_f.at[d],
            recv_sem=recv_f.at[d],
            device_id={"freq": lax.rem(mf + d, nf)},
            device_id_type=MESH,
        )
        copy.start()
        copies.append(copy)
    member = lax.broadcasted_iota(jnp.int32, (LANES, sources), 0) == parcel_ref[...]
    onehot = jnp.where(member, 1.0, 0.0)
    total = here
    for d in range(1, nf):
        copies[d - 1].wait_recv()
        total = total + bin_land[d][0:1, :]
    relative = power / (total / (bins * nf))
    stacked = jnp.concatenate([relative, jnp.ones((8 - bins, sources), jnp.float32)], axis=0)
    sums = dot_t(stacked, onehot)
    part[...] = sums
    again = []
    for d in range(1, ns):
        copy = pltpu.make_async_remote_copy(
            src_ref=part,
            dst_ref=part_land.at[d],
            send_sem=send_s.at[d],
            recv_sem=recv_s.at[d],
            device_id={"src": lax.rem(ms + d, ns)},
            device_id_type=MESH,
        )
        copy.start()
        again.append(copy)
    part_land[0] = sums
    for d in range(1, ns):
        again[d - 1].wait_recv()
    whole = jnp.zeros_like(sums)
    for place in range(ns):
        whole = whole + part_land[lax.rem(ms - place + ns, ns)]
    for copy in copies + again:
        copy.wait_send()
    out_ref[...] = whole[0:bins, 0:PARCELS] / whole[bins : bins + 1, 0:PARCELS]


def parcel_power(power, parcel, nf, ns):
    bins, sources = power.shape
    return pl.pallas_call(
        functools.partial(parcel_kernel, nf, ns),
        out_shape=jax.ShapeDtypeStruct((bins, PARCELS), jnp.float32),
        in_specs=[pl.BlockSpec(memory_space=pltpu.VMEM)] * 2,
        out_specs=pl.BlockSpec(memory_space=pltpu.VMEM),
        scratch_shapes=[
            pltpu.VMEM((8, sources), jnp.float32),
            pltpu.VMEM((nf, 8, sources), jnp.float32),
            pltpu.VMEM((8, LANES), jnp.float32),
            pltpu.VMEM((ns, 8, LANES), jnp.float32),
            pltpu.SemaphoreType.DMA((nf,)),
            pltpu.SemaphoreType.DMA((nf,)),
            pltpu.SemaphoreType.DMA((ns,)),
            pltpu.SemaphoreType.DMA((ns,)),
        ],
        compiler_params=pltpu.CompilerParams(collective_id=1, has_side_effects=True),
        name="parcel_exchange",
    )(power, parcel)


def epoch_rows(spectra, keep):
    bins, parts, channels, epochs = spectra.shape
    kept = keep.astype(jnp.bfloat16)
    masked = spectra * kept
    x = jnp.transpose(masked, (0, 2, 1, 3)).reshape(bins, channels, parts * epochs)
    count = jnp.concatenate([kept, jnp.zeros(((parts - 1) * epochs,), jnp.bfloat16)])
    count = jnp.broadcast_to(count[None, None, :], (bins, 1, parts * epochs))
    rows = blocks_rows(channels)
    spare = jnp.zeros((bins, rows - channels - 1, parts * epochs), jnp.bfloat16)
    return jnp.concatenate([x, count, spare], axis=1)


def local(nf, ns, spectra, keep, lead_field, parcel):
    bins = spectra.shape[0]
    packed = summed_cov(epoch_rows(spectra, keep), ns)
    power = solve(packed, lead_field, bins)
    return power, parcel_power(power, parcel[None, :], nf, ns)


def solution(mesh):
    in_specs = (P("freq", None, None, "src"), P("src"), P(None, None, "src"), P("src"))
    out_specs = (P("freq", "src"), P("freq", None))
    body = functools.partial(local, mesh.shape["freq"], mesh.shape["src"])
    return jax.shard_map(body, mesh=mesh, in_specs=in_specs, out_specs=out_specs, check_vma=False)
```

```python
import functools
import jax
import jax.numpy as jnp
from jax import lax
from jax.experimental import pallas as pl
from jax.experimental.pallas import tpu as pltpu
from jax.sharding import PartitionSpec as P

PARCELS = 68
ridge = 0.05
MESH = pl.DeviceIdType.MESH
HI = lax.Precision.HIGHEST
LANES = 128


def block_plan(rows):
    sizes = [min(LANES, rows - at) for at in range(0, rows, LANES)]
    offsets, total = {}, 0
    for i, size in enumerate(sizes):
        for j in range(i + 1):
            offsets[i, j] = total
            total += size // 8
    return sizes, offsets, total


def cov_kernel(n, chunk, x_ref, out_ref, packed, landing, gathered, send, recv, send2, recv2):
    bins, rows, _ = x_ref.shape
    sizes, offsets, total = block_plan(rows)
    me = lax.axis_index("src")
    barrier = pltpu.get_barrier_semaphore()
    for d in range(1, n):
        pl.semaphore_signal(barrier, inc=1, device_id={"src": lax.rem(me + d, n)}, device_id_type=MESH)
    for f in range(bins):
        for i, size in enumerate(sizes):
            left = x_ref[f, i * LANES : i * LANES + size, :]
            for j in range(i + 1):
                width = sizes[j]
                right = x_ref[f, j * LANES : j * LANES + width, :]
                block = lax.dot_general(left, right, (((1,), (1,)), ((), ())), preferred_element_type=jnp.float32)
                if width < LANES:
                    block = jnp.concatenate([block, jnp.zeros((size, LANES - width), jnp.float32)], axis=1)
                at = f * total + offsets[i, j]
                packed[at : at + size // 8] = block.reshape(size // 8, 8, LANES)
    spare = n * chunk - bins * total
    if spare:
        packed[bins * total :] = jnp.zeros((spare, 8, LANES), jnp.float32)
    pl.semaphore_wait(barrier, n - 1)
    copies = []
    for d in range(1, n):
        to = lax.rem(me + d, n)
        copy = pltpu.make_async_remote_copy(
            src_ref=packed.at[pl.ds(to * chunk, chunk)],
            dst_ref=landing.at[d],
            send_sem=send.at[d],
            recv_sem=recv.at[d],
            device_id={"src": to},
            device_id_type=MESH,
        )
        copy.start()
        copies.append(copy)
    acc = packed[pl.ds(me * chunk, chunk)]
    for d in range(1, n):
        copies[d - 1].wait_recv()
        acc = acc + landing[d]
    gathered[pl.ds(me * chunk, chunk)] = acc
    again = []
    for d in range(1, n):
        to = lax.rem(me + d, n)
        copy = pltpu.make_async_remote_copy(
            src_ref=gathered.at[pl.ds(me * chunk, chunk)],
            dst_ref=gathered.at[pl.ds(me * chunk, chunk)],
            send_sem=send2.at[d],
            recv_sem=recv2.at[d],
            device_id={"src": to},
            device_id_type=MESH,
        )
        copy.start()
        again.append(copy)
    for d in range(1, n):
        again[d - 1].wait_recv()
    for d in range(1, n):
        copies[d - 1].wait_send()
        again[d - 1].wait_send()
    out_ref[...] = gathered[...]


def summed_cov(x, n):
    bins, rows, _ = x.shape
    total = block_plan(rows)[2] * bins
    chunk = -(-total // n)
    full = (n * chunk, 8, LANES)
    return pl.pallas_call(
        functools.partial(cov_kernel, n, chunk),
        out_shape=jax.ShapeDtypeStruct(full, jnp.float32),
        in_specs=[pl.BlockSpec(memory_space=pltpu.VMEM)],
        out_specs=pl.BlockSpec(memory_space=pltpu.VMEM),
        scratch_shapes=[
            pltpu.VMEM(full, jnp.float32),
            pltpu.VMEM((n, chunk, 8, LANES), jnp.float32),
            pltpu.VMEM(full, jnp.float32),
            pltpu.SemaphoreType.DMA((n,)),
            pltpu.SemaphoreType.DMA((n,)),
            pltpu.SemaphoreType.DMA((n,)),
            pltpu.SemaphoreType.DMA((n,)),
        ],
        compiler_params=pltpu.CompilerParams(collective_id=0, has_side_effects=True),
        name="cov_exchange",
    )(x)


def split3(x):
    high = x.astype(jnp.bfloat16).astype(jnp.float32)
    rest = x - high
    middle = rest.astype(jnp.bfloat16).astype(jnp.float32)
    return high, middle, rest - middle


def panels(ps):
    lane = lax.broadcasted_iota(jnp.int32, (8, LANES), 1)
    row = lax.broadcasted_iota(jnp.int32, (8, LANES), 0)
    for k in range(8):
        done = []
        for p in ps:
            col = jnp.where(row >= k, jnp.broadcast_to(p[:, k : k + 1], (8, LANES)), 0.0)
            pivot = jnp.broadcast_to(col[k : k + 1, :], (8, LANES))
            line = jnp.where(lane == k, 1.0, jnp.broadcast_to(p[k : k + 1, :], (8, LANES)))
            scale = lax.rsqrt(pivot)
            scale = scale * (1.5 - (0.5 * pivot) * (scale * scale))
            line = line * scale
            step = col * scale
            below = jnp.where((lane == k) & (row > k), 0.0, p) - step * line
            done.append(jnp.where(row > k, below, jnp.where(row == k, line, p)))
        ps = done
    return [jnp.where((lane < 8) & (lane > row), 0.0, p) for p in ps]


def invert_factors(work, bins, size):
    lane = lax.broadcasted_iota(jnp.int32, (8, LANES), 1)
    rest_lane = lax.broadcasted_iota(jnp.int32, (size - 8, LANES), 1)

    def body(t, carry):
        us = panels([work[f, 0:8, :] for f in range(bins)])
        updates = []
        for u in us:
            ahead = jnp.where((lane >= 8) & (lane < size - 8 * t), u, 0.0)
            ah, am, al = split3(ahead)
            uh, um, ul = split3(u)
            left = jnp.concatenate([ah, ah, am, ah, am, al], axis=0).astype(jnp.bfloat16)
            right = jnp.concatenate([uh, um, uh, ul, um, uh], axis=0).astype(jnp.bfloat16)
            updates.append(
                lax.dot_general(left, right, (((0,), (0,)), ((), ())), preferred_element_type=jnp.float32)
            )
        below = [jnp.where(rest_lane < 8, 0.0, work[f, 8:size, :]) - updates[f][8:size, :] for f in range(bins)]
        below = [pltpu.roll(x, LANES - 8, axis=1) for x in below]
        last = [pltpu.roll(u, LANES - 8, axis=1) for u in us]
        for f in range(bins):
            work[f, 0 : size - 8, :] = below[f]
            work[f, size - 8 : size, :] = last[f]
        return carry

    lax.fori_loop(0, size // 8, body, 0)
    if size < LANES:
        for f in range(bins):
            work[f, 0:size, :] = pltpu.roll(work[f, 0:size, :], size, axis=1)


def dot(a, b):
    return jnp.dot(a, b, precision=HI, preferred_element_type=jnp.float32)


def dot_t(a, b):
    return lax.dot_general(a, b, (((1,), (1,)), ((), ())), precision=HI, preferred_element_type=jnp.float32)


def solve_kernel(bins, packed_ref, lead_ref, out_ref, blocks, work, white, tail):
    channels, sources = lead_ref.shape[1], lead_ref.shape[2]
    rows = blocks_rows(channels)
    sizes, offsets, total = block_plan(rows)
    count = len(sizes)
    for f in range(bins):
        def raw(i, j):
            at = f * total + offsets[i, j]
            return packed_ref[at : at + sizes[i] // 8].reshape(sizes[i], LANES)

        spot = f * total + offsets[count - 1, count - 1]
        edge = channels - (count - 1) * LANES
        kept = packed_ref[spot + edge // 8][edge % 8 : edge % 8 + 1, edge : edge + 1]
        inverse_kept = 1.0 / kept
        eyes, trace = [], jnp.zeros((1, 1), jnp.float32)
        for i, size in enumerate(sizes):
            r = lax.broadcasted_iota(jnp.int32, (size, LANES), 0)
            c = lax.broadcasted_iota(jnp.int32, (size, LANES), 1)
            inside = r + i * LANES < channels
            diagonal = jnp.where((r == c) & inside, raw(i, i), 0.0)
            trace = trace + jnp.sum(jnp.sum(diagonal, axis=0, keepdims=True), axis=1, keepdims=True)
        add = ridge * (trace * inverse_kept) / channels
        for i, size in enumerate(sizes):
            r = lax.broadcasted_iota(jnp.int32, (size, LANES), 0)
            c = lax.broadcasted_iota(jnp.int32, (size, LANES), 1)
            inside = r + i * LANES < channels
            for j in range(i + 1):
                value = raw(i, j) * inverse_kept
                value = jnp.where(inside & (c + j * LANES < channels), value, 0.0)
                if i == j:
                    value = value + jnp.where(r == c, jnp.where(inside, add, 1.0), 0.0)
                blocks[f, i, j, 0:size, :] = value

    tail[...] = jnp.zeros_like(tail)
    for o in range(3):
        tail[0 : channels - (count - 1) * LANES, o * sources : (o + 1) * sources] = lead_ref[o, (count - 1) * LANES : channels, :]

    def lead_block(i):
        if i == count - 1:
            return tail[...]
        return jnp.concatenate([lead_ref[o, i * LANES : (i + 1) * LANES, :] for o in range(3)], axis=1)

    for i, size in enumerate(sizes):
        for f in range(bins):
            work[f, 0:size, :] = blocks[f, i, i, 0:size, :]
        invert_factors(work, bins, size)
        for f in range(bins):
            inverse = work[f, 0:size, 0:size]
            for j in range(i + 1, count):
                blocks[f, j, i, 0 : sizes[j], :] = dot_t(blocks[f, j, i, 0 : sizes[j], :], inverse)
            for j in range(i + 1, count):
                for k in range(i + 1, j + 1):
                    low, high = blocks[f, j, i, 0 : sizes[j], :], blocks[f, k, i, 0 : sizes[k], :]
                    blocks[f, j, k, 0 : sizes[j], 0 : sizes[k]] = blocks[f, j, k, 0 : sizes[j], 0 : sizes[k]] - dot_t(low, high)
            column = lead_block(i)
            for j in range(i):
                column = column - dot(blocks[f, i, j, 0:size, :], white[f, j * LANES : (j + 1) * LANES, :])
            white[f, i * LANES : i * LANES + size, :] = dot(inverse, column)
    for f in range(bins):
        gram = {}
        for a in range(3):
            for b in range(a, 3):
                wa = white[f, :, a * sources : (a + 1) * sources]
                wb = white[f, :, b * sources : (b + 1) * sources]
                gram[a, b] = jnp.sum(wa * wb, axis=0, keepdims=True)
        xx, xy, xz, yy, yz, zz = gram[0, 0], gram[0, 1], gram[0, 2], gram[1, 1], gram[1, 2], gram[2, 2]
        minor_xx = yy * zz - yz * yz
        minor_yy = xx * zz - xz * xz
        minor_zz = xx * yy - xy * xy
        determinant = xx * minor_xx - xy * (xy * zz - yz * xz) + xz * (xy * yz - yy * xz)
        out_ref[f : f + 1, :] = (minor_xx + minor_yy + minor_zz) / determinant


def blocks_rows(channels):
    return -(-(channels + 1) // 16) * 16


def solve(packed, lead_field, bins):
    channels, sources = lead_field.shape[1:]
    rows = blocks_rows(channels)
    sizes, _, _ = block_plan(rows)
    count = len(sizes)
    return pl.pallas_call(
        functools.partial(solve_kernel, bins),
        out_shape=jax.ShapeDtypeStruct((bins, sources), jnp.float32),
        in_specs=[pl.BlockSpec(memory_space=pltpu.VMEM)] * 2,
        out_specs=pl.BlockSpec(memory_space=pltpu.VMEM),
        scratch_shapes=[
            pltpu.VMEM((bins, count, count, LANES, LANES), jnp.float32),
            pltpu.VMEM((bins, LANES, LANES), jnp.float32),
            pltpu.VMEM((bins, rows, 3 * sources), jnp.float32),
            pltpu.VMEM((sizes[-1], 3 * sources), jnp.float32),
        ],
        name="factor_whiten",
    )(packed, lead_field)


def parcel_kernel(nf, ns, power_ref, parcel_ref, out_ref, mine, bin_land, part, part_land, send_f, recv_f, send_s, recv_s):
    bins, sources = power_ref.shape
    mf, ms = lax.axis_index("freq"), lax.axis_index("src")
    barrier = pltpu.get_barrier_semaphore()
    for d in range(1, nf):
        pl.semaphore_signal(barrier, inc=1, device_id={"freq": lax.rem(mf + d, nf)}, device_id_type=MESH)
    for d in range(1, ns):
        pl.semaphore_signal(barrier, inc=1, device_id={"src": lax.rem(ms + d, ns)}, device_id_type=MESH)
    power = power_ref[...]
    here = jnp.sum(power, axis=0, keepdims=True)
    mine[...] = jnp.broadcast_to(here, mine.shape)
    pl.semaphore_wait(barrier, nf + ns - 2)
    copies = []
    for d in range(1, nf):
        copy = pltpu.make_async_remote_copy(
            src_ref=mine,
            dst_ref=bin_land.at[d],
            send_sem=send_f.at[d],
            recv_sem=recv_f.at[d],
            device_id={"freq": lax.rem(mf + d, nf)},
            device_id_type=MESH,
        )
        copy.start()
        copies.append(copy)
    member = lax.broadcasted_iota(jnp.int32, (LANES, sources), 0) == parcel_ref[...]
    onehot = jnp.where(member, 1.0, 0.0)
    total = here
    for d in range(1, nf):
        copies[d - 1].wait_recv()
        total = total + bin_land[d][0:1, :]
    relative = power / (total / (bins * nf))
    stacked = jnp.concatenate([relative, jnp.ones((8 - bins, sources), jnp.float32)], axis=0)
    sums = dot_t(stacked, onehot)
    part[...] = sums
    again = []
    for d in range(1, ns):
        copy = pltpu.make_async_remote_copy(
            src_ref=part,
            dst_ref=part_land.at[d],
            send_sem=send_s.at[d],
            recv_sem=recv_s.at[d],
            device_id={"src": lax.rem(ms + d, ns)},
            device_id_type=MESH,
        )
        copy.start()
        again.append(copy)
    part_land[0] = sums
    for d in range(1, ns):
        again[d - 1].wait_recv()
    whole = jnp.zeros_like(sums)
    for place in range(ns):
        whole = whole + part_land[lax.rem(ms - place + ns, ns)]
    for copy in copies + again:
        copy.wait_send()
    out_ref[...] = whole[0:bins, 0:PARCELS] / whole[bins : bins + 1, 0:PARCELS]


def parcel_power(power, parcel, nf, ns):
    bins, sources = power.shape
    return pl.pallas_call(
        functools.partial(parcel_kernel, nf, ns),
        out_shape=jax.ShapeDtypeStruct((bins, PARCELS), jnp.float32),
        in_specs=[pl.BlockSpec(memory_space=pltpu.VMEM)] * 2,
        out_specs=pl.BlockSpec(memory_space=pltpu.VMEM),
        scratch_shapes=[
            pltpu.VMEM((8, sources), jnp.float32),
            pltpu.VMEM((nf, 8, sources), jnp.float32),
            pltpu.VMEM((8, LANES), jnp.float32),
            pltpu.VMEM((ns, 8, LANES), jnp.float32),
            pltpu.SemaphoreType.DMA((nf,)),
            pltpu.SemaphoreType.DMA((nf,)),
            pltpu.SemaphoreType.DMA((ns,)),
            pltpu.SemaphoreType.DMA((ns,)),
        ],
        compiler_params=pltpu.CompilerParams(collective_id=1, has_side_effects=True),
        name="parcel_exchange",
    )(power, parcel)


def epoch_rows(spectra, keep):
    bins, parts, channels, epochs = spectra.shape
    kept = keep.astype(jnp.bfloat16)
    masked = spectra * kept
    x = jnp.transpose(masked, (0, 2, 1, 3)).reshape(bins, channels, parts * epochs)
    count = jnp.concatenate([kept, jnp.zeros(((parts - 1) * epochs,), jnp.bfloat16)])
    count = jnp.broadcast_to(count[None, None, :], (bins, 1, parts * epochs))
    rows = blocks_rows(channels)
    spare = jnp.zeros((bins, rows - channels - 1, parts * epochs), jnp.bfloat16)
    return jnp.concatenate([x, count, spare], axis=1)


def local(nf, ns, spectra, keep, lead_field, parcel):
    bins = spectra.shape[0]
    packed = summed_cov(epoch_rows(spectra, keep), ns)
    power = solve(packed, lead_field, bins)
    return power, parcel_power(power, parcel[None, :], nf, ns)


def solution(mesh):
    in_specs = (P("freq", None, None, "src"), P("src"), P(None, None, "src"), P("src"))
    out_specs = (P("freq", "src"), P("freq", None))
    body = functools.partial(local, mesh.shape["freq"], mesh.shape["src"])
    return jax.shard_map(body, mesh=mesh, in_specs=in_specs, out_specs=out_specs, check_vma=False)
```

```python
import functools
import jax
import jax.numpy as jnp
from jax import lax
from jax.experimental import pallas as pl
from jax.experimental.pallas import tpu as pltpu
from jax.sharding import PartitionSpec as P

PARCELS = 68
ridge = 0.05
MESH = pl.DeviceIdType.MESH
HI = lax.Precision.HIGHEST
LANES = 128


def block_plan(rows):
    sizes = [min(LANES, rows - at) for at in range(0, rows, LANES)]
    offsets, total = {}, 0
    for i, size in enumerate(sizes):
        for j in range(i + 1):
            offsets[i, j] = total
            total += size // 8
    return sizes, offsets, total


def cov_kernel(n, chunk, x_ref, out_ref, packed, landing, gathered, send, recv, send2, recv2):
    bins, rows, _ = x_ref.shape
    sizes, offsets, total = block_plan(rows)
    me = lax.axis_index("src")
    barrier = pltpu.get_barrier_semaphore()
    for d in range(1, n):
        pl.semaphore_signal(barrier, inc=1, device_id={"src": lax.rem(me + d, n)}, device_id_type=MESH)
    for f in range(bins):
        for i, size in enumerate(sizes):
            left = x_ref[f, i * LANES : i * LANES + size, :]
            for j in range(i + 1):
                width = sizes[j]
                right = x_ref[f, j * LANES : j * LANES + width, :]
                block = lax.dot_general(left, right, (((1,), (1,)), ((), ())), preferred_element_type=jnp.float32)
                if width < LANES:
                    block = jnp.concatenate([block, jnp.zeros((size, LANES - width), jnp.float32)], axis=1)
                at = f * total + offsets[i, j]
                packed[at : at + size // 8] = block.reshape(size // 8, 8, LANES)
    spare = n * chunk - bins * total
    if spare:
        packed[bins * total :] = jnp.zeros((spare, 8, LANES), jnp.float32)
    pl.semaphore_wait(barrier, n - 1)
    copies = []
    for d in range(1, n):
        to = lax.rem(me + d, n)
        copy = pltpu.make_async_remote_copy(
            src_ref=packed.at[pl.ds(to * chunk, chunk)],
            dst_ref=landing.at[d],
            send_sem=send.at[d],
            recv_sem=recv.at[d],
            device_id={"src": to},
            device_id_type=MESH,
        )
        copy.start()
        copies.append(copy)
    acc = packed[pl.ds(me * chunk, chunk)]
    for d in range(1, n):
        copies[d - 1].wait_recv()
        acc = acc + landing[d]
    gathered[pl.ds(me * chunk, chunk)] = acc
    again = []
    for d in range(1, n):
        to = lax.rem(me + d, n)
        copy = pltpu.make_async_remote_copy(
            src_ref=gathered.at[pl.ds(me * chunk, chunk)],
            dst_ref=gathered.at[pl.ds(me * chunk, chunk)],
            send_sem=send2.at[d],
            recv_sem=recv2.at[d],
            device_id={"src": to},
            device_id_type=MESH,
        )
        copy.start()
        again.append(copy)
    for d in range(1, n):
        again[d - 1].wait_recv()
    for d in range(1, n):
        copies[d - 1].wait_send()
        again[d - 1].wait_send()
    out_ref[...] = gathered[...]


def summed_cov(x, n):
    bins, rows, _ = x.shape
    total = block_plan(rows)[2] * bins
    chunk = -(-total // n)
    full = (n * chunk, 8, LANES)
    return pl.pallas_call(
        functools.partial(cov_kernel, n, chunk),
        out_shape=jax.ShapeDtypeStruct(full, jnp.float32),
        in_specs=[pl.BlockSpec(memory_space=pltpu.VMEM)],
        out_specs=pl.BlockSpec(memory_space=pltpu.VMEM),
        scratch_shapes=[
            pltpu.VMEM(full, jnp.float32),
            pltpu.VMEM((n, chunk, 8, LANES), jnp.float32),
            pltpu.VMEM(full, jnp.float32),
            pltpu.SemaphoreType.DMA((n,)),
            pltpu.SemaphoreType.DMA((n,)),
            pltpu.SemaphoreType.DMA((n,)),
            pltpu.SemaphoreType.DMA((n,)),
        ],
        compiler_params=pltpu.CompilerParams(collective_id=0, has_side_effects=True),
        name="cov_exchange",
    )(x)


def split3(x):
    high = x.astype(jnp.bfloat16).astype(jnp.float32)
    rest = x - high
    middle = rest.astype(jnp.bfloat16).astype(jnp.float32)
    return high, middle, rest - middle


def panels(ps):
    lane = lax.broadcasted_iota(jnp.int32, (8, LANES), 1)
    row = lax.broadcasted_iota(jnp.int32, (8, LANES), 0)
    for k in range(8):
        done = []
        for p in ps:
            col = jnp.where(row >= k, jnp.broadcast_to(p[:, k : k + 1], (8, LANES)), 0.0)
            pivot = jnp.broadcast_to(col[k : k + 1, :], (8, LANES))
            line = jnp.where(lane == k, 1.0, jnp.broadcast_to(p[k : k + 1, :], (8, LANES)))
            scale = lax.rsqrt(pivot)
            scale = scale * (1.5 - (0.5 * pivot) * (scale * scale))
            line = line * scale
            step = col * scale
            below = jnp.where((lane == k) & (row > k), 0.0, p) - step * line
            done.append(jnp.where(row > k, below, jnp.where(row == k, line, p)))
        ps = done
    return [jnp.where((lane < 8) & (lane > row), 0.0, p) for p in ps]


def next_rows(u):
    row = lax.broadcasted_iota(jnp.int32, (8, LANES), 0)
    rows = jnp.zeros((8, LANES), jnp.float32)
    for j in range(8):
        product = jnp.broadcast_to(u[:, 8 + j : 9 + j], (8, LANES)) * u
        rows = jnp.where(row == j, jnp.sum(product, axis=0, keepdims=True), rows)
    return rows


def invert_factors(work, bins, size):
    lane = lax.broadcasted_iota(jnp.int32, (8, LANES), 1)
    rest_lane = lax.broadcasted_iota(jnp.int32, (size - 8, LANES), 1)

    def store(us, updates):
        below = [jnp.where(rest_lane < 8, 0.0, work[f, 8:size, :]) for f in range(bins)]
        if updates is not None:
            below = [x - update[8:size, :] for x, update in zip(below, updates)]
        below = [pltpu.roll(x, LANES - 8, axis=1) for x in below]
        last = [pltpu.roll(u, LANES - 8, axis=1) for u in us]
        for f in range(bins):
            work[f, 0 : size - 8, :] = below[f]
            work[f, size - 8 : size, :] = last[f]

    def body(t, us):
        heads = [jnp.where(lane < 8, 0.0, work[f, 8:16, :]) - next_rows(us[f]) for f in range(bins)]
        updates = []
        for u in us:
            ahead = jnp.where((lane >= 8) & (lane < size - 8 * t), u, 0.0)
            ah, am, al = split3(ahead)
            uh, um, ul = split3(u)
            left = jnp.concatenate([ah, ah, am, ah, am, al], axis=0).astype(jnp.bfloat16)
            right = jnp.concatenate([uh, um, uh, ul, um, uh], axis=0).astype(jnp.bfloat16)
            updates.append(
                lax.dot_general(left, right, (((0,), (0,)), ((), ())), preferred_element_type=jnp.float32)
            )
        coming = panels([pltpu.roll(x, LANES - 8, axis=1) for x in heads])
        store(us, updates)
        return tuple(coming)

    us = lax.fori_loop(0, size // 8 - 1, body, tuple(panels([work[f, 0:8, :] for f in range(bins)])))
    store(us, None)
    if size < LANES:
        for f in range(bins):
            work[f, 0:size, :] = pltpu.roll(work[f, 0:size, :], size, axis=1)


def dot(a, b):
    return jnp.dot(a, b, precision=HI, preferred_element_type=jnp.float32)


def dot_t(a, b):
    return lax.dot_general(a, b, (((1,), (1,)), ((), ())), precision=HI, preferred_element_type=jnp.float32)


def solve_kernel(bins, packed_ref, lead_ref, out_ref, blocks, work, white, tail):
    channels, sources = lead_ref.shape[1], lead_ref.shape[2]
    rows = blocks_rows(channels)
    sizes, offsets, total = block_plan(rows)
    count = len(sizes)
    for f in range(bins):
        def raw(i, j):
            at = f * total + offsets[i, j]
            return packed_ref[at : at + sizes[i] // 8].reshape(sizes[i], LANES)

        spot = f * total + offsets[count - 1, count - 1]
        edge = channels - (count - 1) * LANES
        kept = packed_ref[spot + edge // 8][edge % 8 : edge % 8 + 1, edge : edge + 1]
        inverse_kept = 1.0 / kept
        eyes, trace = [], jnp.zeros((1, 1), jnp.float32)
        for i, size in enumerate(sizes):
            r = lax.broadcasted_iota(jnp.int32, (size, LANES), 0)
            c = lax.broadcasted_iota(jnp.int32, (size, LANES), 1)
            inside = r + i * LANES < channels
            diagonal = jnp.where((r == c) & inside, raw(i, i), 0.0)
            trace = trace + jnp.sum(jnp.sum(diagonal, axis=0, keepdims=True), axis=1, keepdims=True)
        add = ridge * (trace * inverse_kept) / channels
        for i, size in enumerate(sizes):
            r = lax.broadcasted_iota(jnp.int32, (size, LANES), 0)
            c = lax.broadcasted_iota(jnp.int32, (size, LANES), 1)
            inside = r + i * LANES < channels
            for j in range(i + 1):
                value = raw(i, j) * inverse_kept
                value = jnp.where(inside & (c + j * LANES < channels), value, 0.0)
                if i == j:
                    value = value + jnp.where(r == c, jnp.where(inside, add, 1.0), 0.0)
                blocks[f, i, j, 0:size, :] = value

    tail[...] = jnp.zeros_like(tail)
    for o in range(3):
        tail[0 : channels - (count - 1) * LANES, o * sources : (o + 1) * sources] = lead_ref[o, (count - 1) * LANES : channels, :]

    def lead_block(i):
        if i == count - 1:
            return tail[...]
        return jnp.concatenate([lead_ref[o, i * LANES : (i + 1) * LANES, :] for o in range(3)], axis=1)

    for i, size in enumerate(sizes):
        for f in range(bins):
            work[f, 0:size, :] = blocks[f, i, i, 0:size, :]
        invert_factors(work, bins, size)
        for f in range(bins):
            inverse = work[f, 0:size, 0:size]
            for j in range(i + 1, count):
                blocks[f, j, i, 0 : sizes[j], :] = dot_t(blocks[f, j, i, 0 : sizes[j], :], inverse)
            for j in range(i + 1, count):
                for k in range(i + 1, j + 1):
                    low, high = blocks[f, j, i, 0 : sizes[j], :], blocks[f, k, i, 0 : sizes[k], :]
                    blocks[f, j, k, 0 : sizes[j], 0 : sizes[k]] = blocks[f, j, k, 0 : sizes[j], 0 : sizes[k]] - dot_t(low, high)
            column = lead_block(i)
            for j in range(i):
                column = column - dot(blocks[f, i, j, 0:size, :], white[f, j * LANES : (j + 1) * LANES, :])
            white[f, i * LANES : i * LANES + size, :] = dot(inverse, column)
    for f in range(bins):
        gram = {}
        for a in range(3):
            for b in range(a, 3):
                wa = white[f, :, a * sources : (a + 1) * sources]
                wb = white[f, :, b * sources : (b + 1) * sources]
                gram[a, b] = jnp.sum(wa * wb, axis=0, keepdims=True)
        xx, xy, xz, yy, yz, zz = gram[0, 0], gram[0, 1], gram[0, 2], gram[1, 1], gram[1, 2], gram[2, 2]
        minor_xx = yy * zz - yz * yz
        minor_yy = xx * zz - xz * xz
        minor_zz = xx * yy - xy * xy
        determinant = xx * minor_xx - xy * (xy * zz - yz * xz) + xz * (xy * yz - yy * xz)
        out_ref[f : f + 1, :] = (minor_xx + minor_yy + minor_zz) / determinant


def blocks_rows(channels):
    return -(-(channels + 1) // 16) * 16


def solve(packed, lead_field, bins):
    channels, sources = lead_field.shape[1:]
    rows = blocks_rows(channels)
    sizes, _, _ = block_plan(rows)
    count = len(sizes)
    return pl.pallas_call(
        functools.partial(solve_kernel, bins),
        out_shape=jax.ShapeDtypeStruct((bins, sources), jnp.float32),
        in_specs=[pl.BlockSpec(memory_space=pltpu.VMEM)] * 2,
        out_specs=pl.BlockSpec(memory_space=pltpu.VMEM),
        scratch_shapes=[
            pltpu.VMEM((bins, count, count, LANES, LANES), jnp.float32),
            pltpu.VMEM((bins, LANES, LANES), jnp.float32),
            pltpu.VMEM((bins, rows, 3 * sources), jnp.float32),
            pltpu.VMEM((sizes[-1], 3 * sources), jnp.float32),
        ],
        name="factor_whiten",
    )(packed, lead_field)


def parcel_kernel(nf, ns, power_ref, parcel_ref, out_ref, mine, bin_land, part, part_land, send_f, recv_f, send_s, recv_s):
    bins, sources = power_ref.shape
    mf, ms = lax.axis_index("freq"), lax.axis_index("src")
    barrier = pltpu.get_barrier_semaphore()
    for d in range(1, nf):
        pl.semaphore_signal(barrier, inc=1, device_id={"freq": lax.rem(mf + d, nf)}, device_id_type=MESH)
    for d in range(1, ns):
        pl.semaphore_signal(barrier, inc=1, device_id={"src": lax.rem(ms + d, ns)}, device_id_type=MESH)
    power = power_ref[...]
    here = jnp.sum(power, axis=0, keepdims=True)
    mine[...] = jnp.broadcast_to(here, mine.shape)
    pl.semaphore_wait(barrier, nf + ns - 2)
    copies = []
    for d in range(1, nf):
        copy = pltpu.make_async_remote_copy(
            src_ref=mine,
            dst_ref=bin_land.at[d],
            send_sem=send_f.at[d],
            recv_sem=recv_f.at[d],
            device_id={"freq": lax.rem(mf + d, nf)},
            device_id_type=MESH,
        )
        copy.start()
        copies.append(copy)
    member = lax.broadcasted_iota(jnp.int32, (LANES, sources), 0) == parcel_ref[...]
    onehot = jnp.where(member, 1.0, 0.0)
    total = here
    for d in range(1, nf):
        copies[d - 1].wait_recv()
        total = total + bin_land[d][0:1, :]
    relative = power / (total / (bins * nf))
    stacked = jnp.concatenate([relative, jnp.ones((8 - bins, sources), jnp.float32)], axis=0)
    sums = dot_t(stacked, onehot)
    part[...] = sums
    again = []
    for d in range(1, ns):
        copy = pltpu.make_async_remote_copy(
            src_ref=part,
            dst_ref=part_land.at[d],
            send_sem=send_s.at[d],
            recv_sem=recv_s.at[d],
            device_id={"src": lax.rem(ms + d, ns)},
            device_id_type=MESH,
        )
        copy.start()
        again.append(copy)
    part_land[0] = sums
    for d in range(1, ns):
        again[d - 1].wait_recv()
    whole = jnp.zeros_like(sums)
    for place in range(ns):
        whole = whole + part_land[lax.rem(ms - place + ns, ns)]
    for copy in copies + again:
        copy.wait_send()
    out_ref[...] = whole[0:bins, 0:PARCELS] / whole[bins : bins + 1, 0:PARCELS]


def parcel_power(power, parcel, nf, ns):
    bins, sources = power.shape
    return pl.pallas_call(
        functools.partial(parcel_kernel, nf, ns),
        out_shape=jax.ShapeDtypeStruct((bins, PARCELS), jnp.float32),
        in_specs=[pl.BlockSpec(memory_space=pltpu.VMEM)] * 2,
        out_specs=pl.BlockSpec(memory_space=pltpu.VMEM),
        scratch_shapes=[
            pltpu.VMEM((8, sources), jnp.float32),
            pltpu.VMEM((nf, 8, sources), jnp.float32),
            pltpu.VMEM((8, LANES), jnp.float32),
            pltpu.VMEM((ns, 8, LANES), jnp.float32),
            pltpu.SemaphoreType.DMA((nf,)),
            pltpu.SemaphoreType.DMA((nf,)),
            pltpu.SemaphoreType.DMA((ns,)),
            pltpu.SemaphoreType.DMA((ns,)),
        ],
        compiler_params=pltpu.CompilerParams(collective_id=1, has_side_effects=True),
        name="parcel_exchange",
    )(power, parcel)


def epoch_rows(spectra, keep):
    bins, parts, channels, epochs = spectra.shape
    kept = keep.astype(jnp.bfloat16)
    masked = spectra * kept
    x = jnp.transpose(masked, (0, 2, 1, 3)).reshape(bins, channels, parts * epochs)
    count = jnp.concatenate([kept, jnp.zeros(((parts - 1) * epochs,), jnp.bfloat16)])
    count = jnp.broadcast_to(count[None, None, :], (bins, 1, parts * epochs))
    rows = blocks_rows(channels)
    spare = jnp.zeros((bins, rows - channels - 1, parts * epochs), jnp.bfloat16)
    return jnp.concatenate([x, count, spare], axis=1)


def local(nf, ns, spectra, keep, lead_field, parcel):
    bins = spectra.shape[0]
    packed = summed_cov(epoch_rows(spectra, keep), ns)
    power = solve(packed, lead_field, bins)
    return power, parcel_power(power, parcel[None, :], nf, ns)


def solution(mesh):
    in_specs = (P("freq", None, None, "src"), P("src"), P(None, None, "src"), P("src"))
    out_specs = (P("freq", "src"), P("freq", None))
    body = functools.partial(local, mesh.shape["freq"], mesh.shape["src"])
    return jax.shard_map(body, mesh=mesh, in_specs=in_specs, out_specs=out_specs, check_vma=False)
```

```python
import functools
import jax
import jax.numpy as jnp
from jax import lax
from jax.experimental import pallas as pl
from jax.experimental.pallas import tpu as pltpu
from jax.sharding import PartitionSpec as P

PARCELS = 68
ridge = 0.05
MESH = pl.DeviceIdType.MESH
HI = lax.Precision.HIGHEST
LANES = 128


def block_plan(rows):
    sizes = [min(LANES, rows - at) for at in range(0, rows, LANES)]
    offsets, total = {}, 0
    for i, size in enumerate(sizes):
        for j in range(i + 1):
            offsets[i, j] = total
            total += size // 8
    return sizes, offsets, total


def exchange_cov(nf, n, chunk, x_ref, packed, landing, gathered, send, recv, send2, recv2):
    bins, rows, _ = x_ref.shape
    sizes, offsets, total = block_plan(rows)
    me, mf = lax.axis_index("src"), lax.axis_index("freq")
    barrier = pltpu.get_barrier_semaphore()
    for d in range(1, nf):
        pl.semaphore_signal(barrier, inc=1, device_id={"freq": lax.rem(mf + d, nf)}, device_id_type=MESH)
    for d in range(1, n):
        pl.semaphore_signal(barrier, inc=1, device_id={"src": lax.rem(me + d, n)}, device_id_type=MESH)
    for f in range(bins):
        for i, size in enumerate(sizes):
            left = x_ref[f, i * LANES : i * LANES + size, :]
            for j in range(i + 1):
                width = sizes[j]
                right = x_ref[f, j * LANES : j * LANES + width, :]
                block = lax.dot_general(left, right, (((1,), (1,)), ((), ())), preferred_element_type=jnp.float32)
                if width < LANES:
                    block = jnp.concatenate([block, jnp.zeros((size, LANES - width), jnp.float32)], axis=1)
                at = f * total + offsets[i, j]
                packed[at : at + size // 8] = block.reshape(size // 8, 8, LANES)
    spare = n * chunk - bins * total
    if spare:
        packed[bins * total :] = jnp.zeros((spare, 8, LANES), jnp.float32)
    pl.semaphore_wait(barrier, nf + n - 2)
    copies = []
    for d in range(1, n):
        to = lax.rem(me + d, n)
        copy = pltpu.make_async_remote_copy(
            src_ref=packed.at[pl.ds(to * chunk, chunk)],
            dst_ref=landing.at[d],
            send_sem=send.at[d],
            recv_sem=recv.at[d],
            device_id={"src": to},
            device_id_type=MESH,
        )
        copy.start()
        copies.append(copy)
    acc = packed[pl.ds(me * chunk, chunk)]
    for d in range(1, n):
        copies[d - 1].wait_recv()
        acc = acc + landing[d]
    gathered[pl.ds(me * chunk, chunk)] = acc
    again = []
    for d in range(1, n):
        to = lax.rem(me + d, n)
        copy = pltpu.make_async_remote_copy(
            src_ref=gathered.at[pl.ds(me * chunk, chunk)],
            dst_ref=gathered.at[pl.ds(me * chunk, chunk)],
            send_sem=send2.at[d],
            recv_sem=recv2.at[d],
            device_id={"src": to},
            device_id_type=MESH,
        )
        copy.start()
        again.append(copy)
    for d in range(1, n):
        again[d - 1].wait_recv()
    for d in range(1, n):
        copies[d - 1].wait_send()
        again[d - 1].wait_send()


def split3(x):
    high = x.astype(jnp.bfloat16).astype(jnp.float32)
    rest = x - high
    middle = rest.astype(jnp.bfloat16).astype(jnp.float32)
    return high, middle, rest - middle


def panels(ps):
    lane = lax.broadcasted_iota(jnp.int32, (8, LANES), 1)
    row = lax.broadcasted_iota(jnp.int32, (8, LANES), 0)
    for k in range(8):
        done = []
        for p in ps:
            col = jnp.where(row >= k, jnp.broadcast_to(p[:, k : k + 1], (8, LANES)), 0.0)
            pivot = jnp.broadcast_to(col[k : k + 1, :], (8, LANES))
            line = jnp.where(lane == k, 1.0, jnp.broadcast_to(p[k : k + 1, :], (8, LANES)))
            scale = lax.rsqrt(pivot)
            scale = scale * (1.5 - (0.5 * pivot) * (scale * scale))
            line = line * scale
            step = col * scale
            below = jnp.where((lane == k) & (row > k), 0.0, p) - step * line
            done.append(jnp.where(row > k, below, jnp.where(row == k, line, p)))
        ps = done
    return [jnp.where((lane < 8) & (lane > row), 0.0, p) for p in ps]


def next_rows(u):
    row = lax.broadcasted_iota(jnp.int32, (8, LANES), 0)
    rows = jnp.zeros((8, LANES), jnp.float32)
    for j in range(8):
        product = jnp.broadcast_to(u[:, 8 + j : 9 + j], (8, LANES)) * u
        rows = jnp.where(row == j, jnp.sum(product, axis=0, keepdims=True), rows)
    return rows


def invert_factors(work, bins, size):
    lane = lax.broadcasted_iota(jnp.int32, (8, LANES), 1)
    rest_lane = lax.broadcasted_iota(jnp.int32, (size - 8, LANES), 1)

    def store(us, updates):
        below = [jnp.where(rest_lane < 8, 0.0, work[f, 8:size, :]) for f in range(bins)]
        if updates is not None:
            below = [x - update[8:size, :] for x, update in zip(below, updates)]
        below = [pltpu.roll(x, LANES - 8, axis=1) for x in below]
        last = [pltpu.roll(u, LANES - 8, axis=1) for u in us]
        for f in range(bins):
            work[f, 0 : size - 8, :] = below[f]
            work[f, size - 8 : size, :] = last[f]

    def body(t, us):
        heads = [jnp.where(lane < 8, 0.0, work[f, 8:16, :]) - next_rows(us[f]) for f in range(bins)]
        updates = []
        for u in us:
            ahead = jnp.where((lane >= 8) & (lane < size - 8 * t), u, 0.0)
            ah, am, al = split3(ahead)
            uh, um, ul = split3(u)
            left = jnp.concatenate([ah, ah, am, ah, am, al], axis=0).astype(jnp.bfloat16)
            right = jnp.concatenate([uh, um, uh, ul, um, uh], axis=0).astype(jnp.bfloat16)
            updates.append(
                lax.dot_general(left, right, (((0,), (0,)), ((), ())), preferred_element_type=jnp.float32)
            )
        coming = panels([pltpu.roll(x, LANES - 8, axis=1) for x in heads])
        store(us, updates)
        return tuple(coming)

    us = lax.fori_loop(0, size // 8 - 1, body, tuple(panels([work[f, 0:8, :] for f in range(bins)])))
    store(us, None)
    if size < LANES:
        for f in range(bins):
            work[f, 0:size, :] = pltpu.roll(work[f, 0:size, :], size, axis=1)


def dot(a, b):
    return jnp.dot(a, b, precision=HI, preferred_element_type=jnp.float32)


def dot_t(a, b):
    return lax.dot_general(a, b, (((1,), (1,)), ((), ())), precision=HI, preferred_element_type=jnp.float32)


def solve_kernel(bins, packed_ref, lead_ref, out_ref, blocks, work, white, tail):
    channels, sources = lead_ref.shape[1], lead_ref.shape[2]
    rows = blocks_rows(channels)
    sizes, offsets, total = block_plan(rows)
    count = len(sizes)
    for f in range(bins):
        def raw(i, j):
            at = f * total + offsets[i, j]
            return packed_ref[at : at + sizes[i] // 8].reshape(sizes[i], LANES)

        spot = f * total + offsets[count - 1, count - 1]
        edge = channels - (count - 1) * LANES
        kept = packed_ref[spot + edge // 8][edge % 8 : edge % 8 + 1, edge : edge + 1]
        inverse_kept = 1.0 / kept
        eyes, trace = [], jnp.zeros((1, 1), jnp.float32)
        for i, size in enumerate(sizes):
            r = lax.broadcasted_iota(jnp.int32, (size, LANES), 0)
            c = lax.broadcasted_iota(jnp.int32, (size, LANES), 1)
            inside = r + i * LANES < channels
            diagonal = jnp.where((r == c) & inside, raw(i, i), 0.0)
            trace = trace + jnp.sum(jnp.sum(diagonal, axis=0, keepdims=True), axis=1, keepdims=True)
        add = ridge * (trace * inverse_kept) / channels
        for i, size in enumerate(sizes):
            r = lax.broadcasted_iota(jnp.int32, (size, LANES), 0)
            c = lax.broadcasted_iota(jnp.int32, (size, LANES), 1)
            inside = r + i * LANES < channels
            for j in range(i + 1):
                value = raw(i, j) * inverse_kept
                value = jnp.where(inside & (c + j * LANES < channels), value, 0.0)
                if i == j:
                    value = value + jnp.where(r == c, jnp.where(inside, add, 1.0), 0.0)
                blocks[f, i, j, 0:size, :] = value

    tail[...] = jnp.zeros_like(tail)
    for o in range(3):
        tail[0 : channels - (count - 1) * LANES, o * sources : (o + 1) * sources] = lead_ref[o, (count - 1) * LANES : channels, :]

    def lead_block(i):
        if i == count - 1:
            return tail[...]
        return jnp.concatenate([lead_ref[o, i * LANES : (i + 1) * LANES, :] for o in range(3)], axis=1)

    for i, size in enumerate(sizes):
        for f in range(bins):
            work[f, 0:size, :] = blocks[f, i, i, 0:size, :]
        invert_factors(work, bins, size)
        for f in range(bins):
            inverse = work[f, 0:size, 0:size]
            for j in range(i + 1, count):
                blocks[f, j, i, 0 : sizes[j], :] = dot_t(blocks[f, j, i, 0 : sizes[j], :], inverse)
            for j in range(i + 1, count):
                for k in range(i + 1, j + 1):
                    low, high = blocks[f, j, i, 0 : sizes[j], :], blocks[f, k, i, 0 : sizes[k], :]
                    blocks[f, j, k, 0 : sizes[j], 0 : sizes[k]] = blocks[f, j, k, 0 : sizes[j], 0 : sizes[k]] - dot_t(low, high)
            column = lead_block(i)
            for j in range(i):
                column = column - dot(blocks[f, i, j, 0:size, :], white[f, j * LANES : (j + 1) * LANES, :])
            white[f, i * LANES : i * LANES + size, :] = dot(inverse, column)
    for f in range(bins):
        gram = {}
        for a in range(3):
            for b in range(a, 3):
                wa = white[f, :, a * sources : (a + 1) * sources]
                wb = white[f, :, b * sources : (b + 1) * sources]
                gram[a, b] = jnp.sum(wa * wb, axis=0, keepdims=True)
        xx, xy, xz, yy, yz, zz = gram[0, 0], gram[0, 1], gram[0, 2], gram[1, 1], gram[1, 2], gram[2, 2]
        minor_xx = yy * zz - yz * yz
        minor_yy = xx * zz - xz * xz
        minor_zz = xx * yy - xy * xy
        determinant = xx * minor_xx - xy * (xy * zz - yz * xz) + xz * (xy * yz - yy * xz)
        out_ref[f : f + 1, :] = (minor_xx + minor_yy + minor_zz) / determinant


def blocks_rows(channels):
    return -(-(channels + 1) // 16) * 16


def exchange_parcels(nf, ns, power_ref, parcel_ref, out_ref, mine, bin_land, part, part_land, send_f, recv_f, send_s, recv_s):
    bins, sources = power_ref.shape
    mf, ms = lax.axis_index("freq"), lax.axis_index("src")
    power = power_ref[...]
    here = jnp.sum(power, axis=0, keepdims=True)
    mine[...] = jnp.broadcast_to(here, mine.shape)
    copies = []
    for d in range(1, nf):
        copy = pltpu.make_async_remote_copy(
            src_ref=mine,
            dst_ref=bin_land.at[d],
            send_sem=send_f.at[d],
            recv_sem=recv_f.at[d],
            device_id={"freq": lax.rem(mf + d, nf)},
            device_id_type=MESH,
        )
        copy.start()
        copies.append(copy)
    member = lax.broadcasted_iota(jnp.int32, (LANES, sources), 0) == parcel_ref[...]
    onehot = jnp.where(member, 1.0, 0.0)
    total = here
    for d in range(1, nf):
        copies[d - 1].wait_recv()
        total = total + bin_land[d][0:1, :]
    relative = power / (total / (bins * nf))
    stacked = jnp.concatenate([relative, jnp.ones((8 - bins, sources), jnp.float32)], axis=0)
    sums = dot_t(stacked, onehot)
    part[...] = sums
    again = []
    for d in range(1, ns):
        copy = pltpu.make_async_remote_copy(
            src_ref=part,
            dst_ref=part_land.at[d],
            send_sem=send_s.at[d],
            recv_sem=recv_s.at[d],
            device_id={"src": lax.rem(ms + d, ns)},
            device_id_type=MESH,
        )
        copy.start()
        again.append(copy)
    part_land[0] = sums
    for d in range(1, ns):
        again[d - 1].wait_recv()
    whole = jnp.zeros_like(sums)
    for place in range(ns):
        whole = whole + part_land[lax.rem(ms - place + ns, ns)]
    for copy in copies + again:
        copy.wait_send()
    out_ref[...] = whole[0:bins, 0:PARCELS] / whole[bins : bins + 1, 0:PARCELS]


def whole_kernel(nf, ns, chunk, x_ref, lead_hbm, parcel_ref, power_ref, out_ref, lead, lead_sem, *scratch):
    load = pltpu.make_async_copy(lead_hbm, lead, lead_sem)
    load.start()
    exchange_cov(nf, ns, chunk, x_ref, *scratch[:7])
    load.wait()
    solve_kernel(x_ref.shape[0], scratch[2], lead, power_ref, *scratch[7:11])
    exchange_parcels(nf, ns, power_ref, parcel_ref, out_ref, *scratch[11:])


def beamform(x, lead_field, parcel, nf, ns):
    channels, sources = lead_field.shape[1:]
    bins, rows, _ = x.shape
    sizes, _, total = block_plan(rows)
    count = len(sizes)
    chunk = -(-bins * total // ns)
    full = (ns * chunk, 8, LANES)
    dma = pltpu.SemaphoreType.DMA
    vmem = pl.BlockSpec(memory_space=pltpu.VMEM)
    return pl.pallas_call(
        functools.partial(whole_kernel, nf, ns, chunk),
        out_shape=[
            jax.ShapeDtypeStruct((bins, sources), jnp.float32),
            jax.ShapeDtypeStruct((bins, PARCELS), jnp.float32),
        ],
        in_specs=[vmem, pl.BlockSpec(memory_space=pl.ANY), vmem],
        out_specs=[vmem, vmem],
        scratch_shapes=[
            pltpu.VMEM(lead_field.shape, jnp.float32),
            dma(()),
            pltpu.VMEM(full, jnp.float32),
            pltpu.VMEM((ns, chunk, 8, LANES), jnp.float32),
            pltpu.VMEM(full, jnp.float32),
            dma((ns,)),
            dma((ns,)),
            dma((ns,)),
            dma((ns,)),
            pltpu.VMEM((bins, count, count, LANES, LANES), jnp.float32),
            pltpu.VMEM((bins, LANES, LANES), jnp.float32),
            pltpu.VMEM((bins, rows, 3 * sources), jnp.float32),
            pltpu.VMEM((sizes[-1], 3 * sources), jnp.float32),
            pltpu.VMEM((8, sources), jnp.float32),
            pltpu.VMEM((nf, 8, sources), jnp.float32),
            pltpu.VMEM((8, LANES), jnp.float32),
            pltpu.VMEM((ns, 8, LANES), jnp.float32),
            dma((nf,)),
            dma((nf,)),
            dma((ns,)),
            dma((ns,)),
        ],
        compiler_params=pltpu.CompilerParams(collective_id=0, has_side_effects=True),
        name="beamform",
    )(x, lead_field, parcel)


def epoch_rows(spectra, keep):
    bins, parts, channels, epochs = spectra.shape
    kept = keep.astype(jnp.bfloat16)
    masked = spectra * kept
    x = jnp.transpose(masked, (0, 2, 1, 3)).reshape(bins, channels, parts * epochs)
    count = jnp.concatenate([kept, jnp.zeros(((parts - 1) * epochs,), jnp.bfloat16)])
    count = jnp.broadcast_to(count[None, None, :], (bins, 1, parts * epochs))
    rows = blocks_rows(channels)
    spare = jnp.zeros((bins, rows - channels - 1, parts * epochs), jnp.bfloat16)
    return jnp.concatenate([x, count, spare], axis=1)


def local(nf, ns, spectra, keep, lead_field, parcel):
    power, parcels = beamform(epoch_rows(spectra, keep), lead_field, parcel[None, :], nf, ns)
    return power, parcels


def solution(mesh):
    in_specs = (P("freq", None, None, "src"), P("src"), P(None, None, "src"), P("src"))
    out_specs = (P("freq", "src"), P("freq", None))
    body = functools.partial(local, mesh.shape["freq"], mesh.shape["src"])
    return jax.shard_map(body, mesh=mesh, in_specs=in_specs, out_specs=out_specs, check_vma=False)
```

```python
import functools
import jax
import jax.numpy as jnp
from jax import lax
from jax.experimental import pallas as pl
from jax.experimental.pallas import tpu as pltpu
from jax.sharding import PartitionSpec as P

PARCELS = 68
ridge = 0.05
MESH = pl.DeviceIdType.MESH
HI = lax.Precision.HIGHEST
LANES = 128


def block_plan(rows):
    sizes = [min(LANES, rows - at) for at in range(0, rows, LANES)]
    offsets, total = {}, 0
    for i, size in enumerate(sizes):
        for j in range(i + 1):
            offsets[i, j] = total
            total += size // 8
    return sizes, offsets, total


def exchange_cov(nf, n, chunk, x_ref, packed, landing, gathered, send, recv, send2, recv2):
    bins, rows, _ = x_ref.shape
    sizes, offsets, total = block_plan(rows)
    me, mf = lax.axis_index("src"), lax.axis_index("freq")
    barrier = pltpu.get_barrier_semaphore()
    for d in range(1, nf):
        pl.semaphore_signal(barrier, inc=1, device_id={"freq": lax.rem(mf + d, nf)}, device_id_type=MESH)
    for d in range(1, n):
        pl.semaphore_signal(barrier, inc=1, device_id={"src": lax.rem(me + d, n)}, device_id_type=MESH)
    for f in range(bins):
        for i, size in enumerate(sizes):
            left = x_ref[f, i * LANES : i * LANES + size, :]
            for j in range(i + 1):
                width = sizes[j]
                right = x_ref[f, j * LANES : j * LANES + width, :]
                block = lax.dot_general(left, right, (((1,), (1,)), ((), ())), preferred_element_type=jnp.float32)
                if width < LANES:
                    block = jnp.concatenate([block, jnp.zeros((size, LANES - width), jnp.float32)], axis=1)
                at = f * total + offsets[i, j]
                packed[at : at + size // 8] = block.reshape(size // 8, 8, LANES)
    spare = n * chunk - bins * total
    if spare:
        packed[bins * total :] = jnp.zeros((spare, 8, LANES), jnp.float32)
    pl.semaphore_wait(barrier, nf + n - 2)
    copies = []
    for d in range(1, n):
        to = lax.rem(me + d, n)
        copy = pltpu.make_async_remote_copy(
            src_ref=packed.at[pl.ds(to * chunk, chunk)],
            dst_ref=landing.at[d],
            send_sem=send.at[d],
            recv_sem=recv.at[d],
            device_id={"src": to},
            device_id_type=MESH,
        )
        copy.start()
        copies.append(copy)
    acc = packed[pl.ds(me * chunk, chunk)]
    for d in range(1, n):
        copies[d - 1].wait_recv()
        acc = acc + landing[d]
    gathered[pl.ds(me * chunk, chunk)] = acc
    again = []
    for d in range(1, n):
        to = lax.rem(me + d, n)
        copy = pltpu.make_async_remote_copy(
            src_ref=gathered.at[pl.ds(me * chunk, chunk)],
            dst_ref=gathered.at[pl.ds(me * chunk, chunk)],
            send_sem=send2.at[d],
            recv_sem=recv2.at[d],
            device_id={"src": to},
            device_id_type=MESH,
        )
        copy.start()
        again.append(copy)
    for d in range(1, n):
        again[d - 1].wait_recv()
    for d in range(1, n):
        copies[d - 1].wait_send()
        again[d - 1].wait_send()


def split3(x):
    high = x.astype(jnp.bfloat16).astype(jnp.float32)
    rest = x - high
    middle = rest.astype(jnp.bfloat16).astype(jnp.float32)
    return high, middle, rest - middle


def panels(ps):
    lane = lax.broadcasted_iota(jnp.int32, (8, LANES), 1)
    row = lax.broadcasted_iota(jnp.int32, (8, LANES), 0)
    spread = [
        [jnp.where(row >= 0, jnp.broadcast_to(p[:, j : j + 1], (8, LANES)), 0.0) for j in range(8)] for p in ps
    ]
    for k in range(8):
        done = []
        for p, cols in zip(ps, spread):
            col = jnp.where(row >= k, cols[k], 0.0)
            pivot = jnp.broadcast_to(col[k : k + 1, :], (8, LANES))
            scale = lax.rsqrt(pivot)
            scale = scale * (1.5 - (0.5 * pivot) * (scale * scale))
            step = col * scale
            for j in range(k + 1, 8):
                cols[j] = cols[j] - step * (jnp.broadcast_to(cols[j][k : k + 1, :], (8, LANES)) * scale)
            line = jnp.where(lane == k, 1.0, jnp.broadcast_to(p[k : k + 1, :], (8, LANES))) * scale
            below = jnp.where((lane == k) & (row > k), 0.0, p) - step * line
            done.append(jnp.where(row > k, below, jnp.where(row == k, line, p)))
        ps = done
    return [jnp.where((lane < 8) & (lane > row), 0.0, p) for p in ps]


def next_rows(u):
    row = lax.broadcasted_iota(jnp.int32, (8, LANES), 0)
    rows = jnp.zeros((8, LANES), jnp.float32)
    for j in range(8):
        product = jnp.broadcast_to(u[:, 8 + j : 9 + j], (8, LANES)) * u
        rows = jnp.where(row == j, jnp.sum(product, axis=0, keepdims=True), rows)
    return rows


def invert_factors(work, bins, size):
    lane = lax.broadcasted_iota(jnp.int32, (8, LANES), 1)
    rest_lane = lax.broadcasted_iota(jnp.int32, (size - 8, LANES), 1)

    def store(us, updates):
        below = [jnp.where(rest_lane < 8, 0.0, work[f, 8:size, :]) for f in range(bins)]
        if updates is not None:
            below = [x - update[8:size, :] for x, update in zip(below, updates)]
        below = [pltpu.roll(x, LANES - 8, axis=1) for x in below]
        last = [pltpu.roll(u, LANES - 8, axis=1) for u in us]
        for f in range(bins):
            work[f, 0 : size - 8, :] = below[f]
            work[f, size - 8 : size, :] = last[f]

    def body(t, us):
        heads = [jnp.where(lane < 8, 0.0, work[f, 8:16, :]) - next_rows(us[f]) for f in range(bins)]
        updates = []
        for u in us:
            ahead = jnp.where((lane >= 8) & (lane < size - 8 * t), u, 0.0)
            ah, am, al = split3(ahead)
            uh, um, ul = split3(u)
            left = jnp.concatenate([ah, ah, am, ah, am, al], axis=0).astype(jnp.bfloat16)
            right = jnp.concatenate([uh, um, uh, ul, um, uh], axis=0).astype(jnp.bfloat16)
            updates.append(
                lax.dot_general(left, right, (((0,), (0,)), ((), ())), preferred_element_type=jnp.float32)
            )
        coming = panels([pltpu.roll(x, LANES - 8, axis=1) for x in heads])
        store(us, updates)
        return tuple(coming)

    us = lax.fori_loop(0, size // 8 - 1, body, tuple(panels([work[f, 0:8, :] for f in range(bins)])))
    store(us, None)
    if size < LANES:
        for f in range(bins):
            work[f, 0:size, :] = pltpu.roll(work[f, 0:size, :], size, axis=1)


def dot(a, b):
    return jnp.dot(a, b, precision=HI, preferred_element_type=jnp.float32)


def dot_t(a, b):
    return lax.dot_general(a, b, (((1,), (1,)), ((), ())), precision=HI, preferred_element_type=jnp.float32)


def solve_kernel(bins, packed_ref, lead_ref, out_ref, blocks, work, white, tail):
    channels, sources = lead_ref.shape[1], lead_ref.shape[2]
    rows = blocks_rows(channels)
    sizes, offsets, total = block_plan(rows)
    count = len(sizes)
    for f in range(bins):
        def raw(i, j):
            at = f * total + offsets[i, j]
            return packed_ref[at : at + sizes[i] // 8].reshape(sizes[i], LANES)

        spot = f * total + offsets[count - 1, count - 1]
        edge = channels - (count - 1) * LANES
        kept = packed_ref[spot + edge // 8][edge % 8 : edge % 8 + 1, edge : edge + 1]
        inverse_kept = 1.0 / kept
        eyes, trace = [], jnp.zeros((1, 1), jnp.float32)
        for i, size in enumerate(sizes):
            r = lax.broadcasted_iota(jnp.int32, (size, LANES), 0)
            c = lax.broadcasted_iota(jnp.int32, (size, LANES), 1)
            inside = r + i * LANES < channels
            diagonal = jnp.where((r == c) & inside, raw(i, i), 0.0)
            trace = trace + jnp.sum(jnp.sum(diagonal, axis=0, keepdims=True), axis=1, keepdims=True)
        add = ridge * (trace * inverse_kept) / channels
        for i, size in enumerate(sizes):
            r = lax.broadcasted_iota(jnp.int32, (size, LANES), 0)
            c = lax.broadcasted_iota(jnp.int32, (size, LANES), 1)
            inside = r + i * LANES < channels
            for j in range(i + 1):
                value = raw(i, j) * inverse_kept
                value = jnp.where(inside & (c + j * LANES < channels), value, 0.0)
                if i == j:
                    value = value + jnp.where(r == c, jnp.where(inside, add, 1.0), 0.0)
                blocks[f, i, j, 0:size, :] = value

    tail[...] = jnp.zeros_like(tail)
    for o in range(3):
        tail[0 : channels - (count - 1) * LANES, o * sources : (o + 1) * sources] = lead_ref[o, (count - 1) * LANES : channels, :]

    def lead_block(i):
        if i == count - 1:
            return tail[...]
        return jnp.concatenate([lead_ref[o, i * LANES : (i + 1) * LANES, :] for o in range(3)], axis=1)

    for i, size in enumerate(sizes):
        for f in range(bins):
            work[f, 0:size, :] = blocks[f, i, i, 0:size, :]
        invert_factors(work, bins, size)
        for f in range(bins):
            inverse = work[f, 0:size, 0:size]
            for j in range(i + 1, count):
                blocks[f, j, i, 0 : sizes[j], :] = dot_t(blocks[f, j, i, 0 : sizes[j], :], inverse)
            for j in range(i + 1, count):
                for k in range(i + 1, j + 1):
                    low, high = blocks[f, j, i, 0 : sizes[j], :], blocks[f, k, i, 0 : sizes[k], :]
                    blocks[f, j, k, 0 : sizes[j], 0 : sizes[k]] = blocks[f, j, k, 0 : sizes[j], 0 : sizes[k]] - dot_t(low, high)
            column = lead_block(i)
            for j in range(i):
                column = column - dot(blocks[f, i, j, 0:size, :], white[f, j * LANES : (j + 1) * LANES, :])
            white[f, i * LANES : i * LANES + size, :] = dot(inverse, column)
    for f in range(bins):
        gram = {}
        for a in range(3):
            for b in range(a, 3):
                wa = white[f, :, a * sources : (a + 1) * sources]
                wb = white[f, :, b * sources : (b + 1) * sources]
                gram[a, b] = jnp.sum(wa * wb, axis=0, keepdims=True)
        xx, xy, xz, yy, yz, zz = gram[0, 0], gram[0, 1], gram[0, 2], gram[1, 1], gram[1, 2], gram[2, 2]
        minor_xx = yy * zz - yz * yz
        minor_yy = xx * zz - xz * xz
        minor_zz = xx * yy - xy * xy
        determinant = xx * minor_xx - xy * (xy * zz - yz * xz) + xz * (xy * yz - yy * xz)
        out_ref[f : f + 1, :] = (minor_xx + minor_yy + minor_zz) / determinant


def blocks_rows(channels):
    return -(-(channels + 1) // 16) * 16


def exchange_parcels(nf, ns, power_ref, parcel_ref, out_ref, mine, bin_land, part, part_land, send_f, recv_f, send_s, recv_s):
    bins, sources = power_ref.shape
    mf, ms = lax.axis_index("freq"), lax.axis_index("src")
    power = power_ref[...]
    here = jnp.sum(power, axis=0, keepdims=True)
    mine[...] = jnp.broadcast_to(here, mine.shape)
    copies = []
    for d in range(1, nf):
        copy = pltpu.make_async_remote_copy(
            src_ref=mine,
            dst_ref=bin_land.at[d],
            send_sem=send_f.at[d],
            recv_sem=recv_f.at[d],
            device_id={"freq": lax.rem(mf + d, nf)},
            device_id_type=MESH,
        )
        copy.start()
        copies.append(copy)
    member = lax.broadcasted_iota(jnp.int32, (LANES, sources), 0) == parcel_ref[...]
    onehot = jnp.where(member, 1.0, 0.0)
    total = here
    for d in range(1, nf):
        copies[d - 1].wait_recv()
        total = total + bin_land[d][0:1, :]
    relative = power / (total / (bins * nf))
    stacked = jnp.concatenate([relative, jnp.ones((8 - bins, sources), jnp.float32)], axis=0)
    sums = dot_t(stacked, onehot)
    part[...] = sums
    again = []
    for d in range(1, ns):
        copy = pltpu.make_async_remote_copy(
            src_ref=part,
            dst_ref=part_land.at[d],
            send_sem=send_s.at[d],
            recv_sem=recv_s.at[d],
            device_id={"src": lax.rem(ms + d, ns)},
            device_id_type=MESH,
        )
        copy.start()
        again.append(copy)
    part_land[0] = sums
    for d in range(1, ns):
        again[d - 1].wait_recv()
    whole = jnp.zeros_like(sums)
    for place in range(ns):
        whole = whole + part_land[lax.rem(ms - place + ns, ns)]
    for copy in copies + again:
        copy.wait_send()
    out_ref[...] = whole[0:bins, 0:PARCELS] / whole[bins : bins + 1, 0:PARCELS]


def whole_kernel(nf, ns, chunk, x_ref, lead_hbm, parcel_ref, power_ref, out_ref, lead, lead_sem, *scratch):
    load = pltpu.make_async_copy(lead_hbm, lead, lead_sem)
    load.start()
    exchange_cov(nf, ns, chunk, x_ref, *scratch[:7])
    load.wait()
    solve_kernel(x_ref.shape[0], scratch[2], lead, power_ref, *scratch[7:11])
    exchange_parcels(nf, ns, power_ref, parcel_ref, out_ref, *scratch[11:])


def beamform(x, lead_field, parcel, nf, ns):
    channels, sources = lead_field.shape[1:]
    bins, rows, _ = x.shape
    sizes, _, total = block_plan(rows)
    count = len(sizes)
    chunk = -(-bins * total // ns)
    full = (ns * chunk, 8, LANES)
    dma = pltpu.SemaphoreType.DMA
    vmem = pl.BlockSpec(memory_space=pltpu.VMEM)
    return pl.pallas_call(
        functools.partial(whole_kernel, nf, ns, chunk),
        out_shape=[
            jax.ShapeDtypeStruct((bins, sources), jnp.float32),
            jax.ShapeDtypeStruct((bins, PARCELS), jnp.float32),
        ],
        in_specs=[vmem, pl.BlockSpec(memory_space=pl.ANY), vmem],
        out_specs=[vmem, vmem],
        scratch_shapes=[
            pltpu.VMEM(lead_field.shape, jnp.float32),
            dma(()),
            pltpu.VMEM(full, jnp.float32),
            pltpu.VMEM((ns, chunk, 8, LANES), jnp.float32),
            pltpu.VMEM(full, jnp.float32),
            dma((ns,)),
            dma((ns,)),
            dma((ns,)),
            dma((ns,)),
            pltpu.VMEM((bins, count, count, LANES, LANES), jnp.float32),
            pltpu.VMEM((bins, LANES, LANES), jnp.float32),
            pltpu.VMEM((bins, rows, 3 * sources), jnp.float32),
            pltpu.VMEM((sizes[-1], 3 * sources), jnp.float32),
            pltpu.VMEM((8, sources), jnp.float32),
            pltpu.VMEM((nf, 8, sources), jnp.float32),
            pltpu.VMEM((8, LANES), jnp.float32),
            pltpu.VMEM((ns, 8, LANES), jnp.float32),
            dma((nf,)),
            dma((nf,)),
            dma((ns,)),
            dma((ns,)),
        ],
        compiler_params=pltpu.CompilerParams(collective_id=0, has_side_effects=True),
        name="beamform",
    )(x, lead_field, parcel)


def epoch_rows(spectra, keep):
    bins, parts, channels, epochs = spectra.shape
    kept = keep.astype(jnp.bfloat16)
    masked = spectra * kept
    x = jnp.transpose(masked, (0, 2, 1, 3)).reshape(bins, channels, parts * epochs)
    count = jnp.concatenate([kept, jnp.zeros(((parts - 1) * epochs,), jnp.bfloat16)])
    count = jnp.broadcast_to(count[None, None, :], (bins, 1, parts * epochs))
    rows = blocks_rows(channels)
    spare = jnp.zeros((bins, rows - channels - 1, parts * epochs), jnp.bfloat16)
    return jnp.concatenate([x, count, spare], axis=1)


def local(nf, ns, spectra, keep, lead_field, parcel):
    power, parcels = beamform(epoch_rows(spectra, keep), lead_field, parcel[None, :], nf, ns)
    return power, parcels


def solution(mesh):
    in_specs = (P("freq", None, None, "src"), P("src"), P(None, None, "src"), P("src"))
    out_specs = (P("freq", "src"), P("freq", None))
    body = functools.partial(local, mesh.shape["freq"], mesh.shape["src"])
    return jax.shard_map(body, mesh=mesh, in_specs=in_specs, out_specs=out_specs, check_vma=False)
```
